32 devices in a mesh: grp: 4 (over y, x), dev: 8 (over z, core).
Axes of the slice: x: 2, y: 2, z: 4, core: 2. Of those that a mesh axis runs over, the one named last changes fastest.
Arguments:
- functions: bfloat16 [6144, 3072], P('dev', 'grp'), may hold values from -6 to 6
- applied: bfloat16 [6144, 3072], P('dev', 'grp'), may hold values from -6 to 6
- kernel: bfloat16 [6144, 768], P('dev'), may hold values from -0.21875 to 0.21875
- live_counts: int32 [8, 8], P('dev'), may hold values from 24 to 96, as said below
- coef_counts: int32 [4, 8], P('grp', 'dev'), may hold values from 192 to 768, as said below
Outputs:
- gradient: bfloat16 [6144, 3072], P('dev', 'grp')
The draws below stay inside these ranges and needn't reach their ends.
Inputs may be any that keep to these rules, and one draw needn't show every extreme that they name: `live_counts`: no owner fills more than 96 slots of a neighborhood; some neighborhood gets 96 live slots from every owner, and some entry is the smallest value. `coef_counts`: some region has all 768 coefficients live, and some has the smallest count.
All inputs are finite; a program needn't handle non-finite values.
Results may differ from the reference program's by a relative error of at most 0.017.
Values may be sent and summed in bfloat16 or wider, within the bound.
A program may use at most 64 MiB of HBM per device.

```python
import jax
import jax.numpy as jnp
from jax import lax

SLOTS = 768
COEF = 768
CAP = 96
N_GRP = 4
N_DEV = 8


def draw_live_counts(key, part):
    lowest = max(1, CAP // 4)
    drawn = jax.random.randint(jax.random.fold_in(key, 11), (N_DEV, N_DEV), lowest, CAP + 1)
    full_row = jax.random.randint(jax.random.fold_in(key, 12), (), 0, N_DEV)
    low_column = jax.random.randint(jax.random.fold_in(key, 13), (), 0, N_DEV)
    row_index = jnp.arange(N_DEV)[:, None]
    column_index = jnp.arange(N_DEV)[None, :]
    drawn = jnp.where(row_index == full_row, CAP, drawn)
    low_row = (full_row + 1) % N_DEV
    drawn = jnp.where((row_index == low_row) & (column_index == low_column), lowest, drawn)
    return drawn.astype(jnp.int32)


def draw_coef_counts(key, part):
    lowest = COEF // 4
    drawn = jax.random.randint(jax.random.fold_in(key, 21), (N_GRP, N_DEV), lowest, COEF + 1)
    flat_index = jnp.arange(N_GRP * N_DEV).reshape(N_GRP, N_DEV)
    full_spot = jax.random.randint(jax.random.fold_in(key, 22), (), 0, N_GRP * N_DEV)
    low_spot = (full_spot + 1 + jax.random.randint(jax.random.fold_in(key, 23), (), 0, N_GRP * N_DEV - 1)) % (N_GRP * N_DEV)
    drawn = jnp.where(flat_index == full_spot, COEF, drawn)
    drawn = jnp.where(flat_index == low_spot, lowest, drawn)
    return drawn.astype(jnp.int32)


def levels(key, dims, pieces, low, high):
    gain = 1.0
    for dim, blocks in pieces:
        steps = jax.random.uniform(jax.random.fold_in(jax.random.fold_in(key, 6), dim), (blocks,), jnp.float32, low / len(pieces), high / len(pieces))
        gain = gain * jnp.repeat(jnp.exp(steps), dims[dim] // blocks).reshape((-1,) + (1,) * (len(dims) - 1 - dim))
    return gain


def normal_values(rng, extent, width, limit, pieces=(), kind=jnp.bfloat16):
    values = jax.random.normal(rng, extent, jnp.float32) * width
    if len(pieces) > 0:
        values = levels(rng, extent, pieces, -0.22, 0.18) * values
    return jnp.clip(values, min=-limit, max=limit).astype(kind)


def setup_inputs(seed: int = 0) -> dict:
    key_list = jax.random.split(jax.random.key(seed), 6)
    return {
        "functions": normal_values(key_list[0], (N_DEV * SLOTS, N_GRP * COEF), 1.0, 6.0, ((0, 8), (1, 4))),
        "applied": normal_values(key_list[1], (N_DEV * SLOTS, N_GRP * COEF), 1.0, 6.0, ((0, 8), (1, 4))),
        "kernel": normal_values(key_list[2], (N_DEV * SLOTS, SLOTS), SLOTS ** -0.5, 0.21875, ((0, 8),)),
        "live_counts": draw_live_counts(jax.random.fold_in(key_list[5], 71), 0),
        "coef_counts": draw_coef_counts(jax.random.fold_in(key_list[5], 71), 0),
    }


def reference(functions, applied, kernel, live_counts, coef_counts):
    per_owner = SLOTS // N_DEV
    shaped_funcs = functions.reshape(N_DEV, N_DEV, per_owner, N_GRP, COEF)
    shaped_applied = applied.reshape(N_DEV, N_DEV, per_owner, N_GRP, COEF)
    kernels = kernel.reshape(N_DEV, SLOTS, SLOTS)
    slot_owner = jnp.arange(SLOTS, dtype=jnp.int32) // per_owner
    slot_rank = jnp.arange(SLOTS, dtype=jnp.int32) % per_owner
    coef_index = jnp.arange(COEF, dtype=jnp.int32)

    def neighborhood(region_index):
        block_funcs = lax.dynamic_index_in_dim(shaped_funcs, region_index, 1, keepdims=False)
        block_funcs = block_funcs.transpose(2, 0, 1, 3).reshape(N_GRP, SLOTS, COEF)
        block_applied = lax.dynamic_index_in_dim(shaped_applied, region_index, 1, keepdims=False)
        block_applied = block_applied.transpose(2, 0, 1, 3).reshape(N_GRP, SLOTS, COEF)
        live_row = lax.dynamic_index_in_dim(live_counts, region_index, 0, keepdims=False)
        slot_live = slot_rank < live_row[slot_owner]
        coef_column = lax.dynamic_index_in_dim(coef_counts, region_index, 1, keepdims=False)
        coef_live = coef_index[None, :] < coef_column[:, None]
        live_mask = slot_live[None, :, None] & coef_live[:, None, :]
        zero_value = jnp.zeros((), jnp.bfloat16)
        masked_funcs = jnp.where(live_mask, block_funcs, zero_value)
        masked_applied = jnp.where(live_mask, block_applied, zero_value)
        partial_value = jnp.einsum("gsc,gtc->gst", masked_funcs.astype(jnp.float32), masked_applied.astype(jnp.float32))
        symmetric = 0.5 * (partial_value + jnp.swapaxes(partial_value, 1, 2))
        hamiltonian = jnp.sum(symmetric, axis=0) / COEF
        ham_rounded = hamiltonian.astype(jnp.bfloat16)
        kernel_here = lax.dynamic_index_in_dim(kernels, region_index, 0, keepdims=False)
        multiplier = jnp.dot(kernel_here, ham_rounded, preferred_element_type=jnp.float32).astype(jnp.bfloat16)
        kernel_part = jnp.einsum("st,gtc->gsc", kernel_here.astype(jnp.float32), masked_applied.astype(jnp.float32))
        multiplier_part = jnp.einsum("st,gtc->gsc", multiplier.astype(jnp.float32), masked_funcs.astype(jnp.float32))
        gradient = jnp.where(live_mask, kernel_part - multiplier_part, jnp.float32(0.0))
        return gradient.astype(jnp.bfloat16)

    result = lax.map(neighborhood, jnp.arange(N_DEV, dtype=jnp.int32))
    result = result.reshape(N_DEV, N_GRP, N_DEV, per_owner, COEF)
    result = result.transpose(2, 0, 3, 1, 4)
    return result.reshape(N_DEV * SLOTS, N_GRP * COEF)
```

```python
import functools

import jax
import jax.numpy as jnp
from jax import lax
from jax.experimental import pallas as pl
from jax.experimental.pallas import tpu as pltpu
from jax.sharding import PartitionSpec as P

MESH = pl.DeviceIdType.MESH
CORES = 2
BANDS = 8


def arrival_orders(chips):
    half = chips // 2
    return [
        sorted(range(chips), key=lambda s: (abs(s - z), (s < half) != (z < half), s)) for z in range(chips)
    ]


def pick(index, values):
    if all(v == values[0] for v in values):
        return values[0]
    found = jnp.int32(values[0])
    for k in range(1, len(values)):
        found = jnp.where(index == k, jnp.int32(values[k]), found)
    return found


def body(
    n_grp, n_dev, live_ref, coef_ref, f_hbm, a_hbm, k_hbm, out_ref,
    land_f, land_a, land_k, fm, am, kp, ka, s_loc, s_in, low, ham, g_buf,
    f_send, f_recv, a_send, a_recv, s_send, s_recv, g_send, g_recv, k_sem, own_sem,
):
    per, coef = f_hbm.shape[1:]
    slots = n_dev * per
    chips = n_dev // CORES
    bands = min(BANDS, n_dev)
    group = n_dev // bands
    rows = group * per
    grp, dev = lax.axis_index("grp"), lax.axis_index("dev")
    chip, core = dev // CORES, dev % CORES
    other = 1 - core
    orders = arrival_orders(chips)

    sources = []
    for p in range(chips):
        z = pick(chip, [orders[k][p] for k in range(chips)])
        sources += [z * CORES + core, z * CORES + other]
    sends = []
    for p in range(1, chips):
        z = pick(chip, [orders[k][p] for k in range(chips)])
        spot = pick(chip, [orders[orders[k][p]].index(k) for k in range(chips)])
        sends += [(z * CORES + core, spot * CORES), (z * CORES + other, spot * CORES + 1)]
    sends.append((chip * CORES + other, 1))

    k_copies = [
        pltpu.make_async_copy(k_hbm.at[sources[i]], land_k.at[i], k_sem.at[i]) for i in range(n_dev)
    ]
    own = [
        pltpu.make_async_copy(f_hbm.at[dev], land_f.at[0], own_sem.at[0]),
        pltpu.make_async_copy(a_hbm.at[dev], land_a.at[0], own_sem.at[1]),
    ]

    barrier = pltpu.get_barrier_semaphore()
    for r in range(1, n_dev):
        pl.semaphore_signal(barrier, inc=1, device_id={"dev": (dev + r) % n_dev}, device_id_type=MESH)
    for r in range(1, n_grp):
        pl.semaphore_signal(barrier, inc=1, device_id={"grp": (grp + r) % n_grp}, device_id_type=MESH)
    for copy in own + k_copies:
        copy.start()
    pl.semaphore_wait(barrier, n_dev + n_grp - 2)

    outgoing = []
    for number, (target, spot) in enumerate(sends):
        for src, dst, ss, rs in ((f_hbm, land_f, f_send, f_recv), (a_hbm, land_a, a_send, a_recv)):
            copy = pltpu.make_async_remote_copy(
                src_ref=src.at[target], dst_ref=dst.at[spot],
                send_sem=ss.at[number], recv_sem=rs.at[spot],
                device_id={"dev": target}, device_id_type=MESH,
            )
            copy.start()
            outgoing.append(copy)

    def flat(ref, band):
        pieces = [ref[band * group + t].astype(jnp.float32) for t in range(group)]
        return jnp.concatenate(pieces, axis=0) if group > 1 else pieces[0]

    def band_slice(band):
        return pl.ds(band * rows, rows)

    column = lax.broadcasted_iota(jnp.int32, (1, slots), 1)
    target_row = jnp.zeros((1, slots), jnp.int32)
    for i in range(n_dev):
        inside = (column >= i * per) & (column < (i + 1) * per)
        target_row = jnp.where(inside, column + (sources[i] - i) * per, target_row)
    onehot = (lax.broadcasted_iota(jnp.int32, (slots, slots), 0) == target_row)
    ham[...] = jnp.where(onehot, jnp.float32(1.0), jnp.float32(0.0)).astype(jnp.bfloat16)
    for copy in k_copies:
        copy.wait()
    for band in range(bands):
        kp[band_slice(band), :] = jnp.dot(
            flat(land_k, band).astype(jnp.bfloat16), ham[...], preferred_element_type=jnp.float32
        ).astype(jnp.bfloat16)

    coef_live = lax.broadcasted_iota(jnp.int32, (rows, coef), 1) < coef_ref[0, 0]
    rank = lax.broadcasted_iota(jnp.int32, (rows, coef), 0)

    def live_mask(band):
        live = None
        for t in range(group):
            count = live_ref[0, sources[band * group + t]]
            inside = (rank >= t * per) & (rank < t * per + jnp.minimum(count, per))
            live = inside if live is None else live | inside
        return live & coef_live

    low[...] = jnp.zeros_like(low)
    contract = (((1,), (1,)), ((), ()))
    tile_sends = []
    for band in range(bands):
        for i in range(band * group, (band + 1) * group):
            if i == 0:
                own[0].wait()
                own[1].wait()
                continue
            for src, dst, ss, rs in ((f_hbm, land_f, f_send, f_recv), (a_hbm, land_a, a_send, a_recv)):
                pltpu.make_async_remote_copy(
                    src_ref=src.at[0], dst_ref=dst.at[i], send_sem=ss.at[0], recv_sem=rs.at[i],
                    device_id={"dev": sources[i]}, device_id_type=MESH,
                ).wait_recv()
        mask = live_mask(band)
        f_new = jnp.where(mask, flat(land_f, band), jnp.float32(0.0)).astype(jnp.bfloat16)
        a_new = jnp.where(mask, flat(land_a, band), jnp.float32(0.0)).astype(jnp.bfloat16)
        fm[band_slice(band), :] = f_new
        am[band_slice(band), :] = a_new
        upto = (band + 1) * rows
        tile = lax.dot_general(f_new, am[0:upto, :], contract, preferred_element_type=jnp.float32)
        tile += lax.dot_general(a_new, fm[0:upto, :], contract, preferred_element_type=jnp.float32)
        low[band_slice(band), 0:upto] = 0.5 * tile
        width = -(-upto // 128) * 128
        s_loc[band, :, 0:width] = low[band_slice(band), 0:width].astype(jnp.bfloat16)
        for r in range(1, n_grp):
            copy = pltpu.make_async_remote_copy(
                src_ref=s_loc.at[band, :, 0:width], dst_ref=s_in.at[r - 1, band, :, 0:width],
                send_sem=s_send.at[r - 1, band], recv_sem=s_recv.at[r - 1, band],
                device_id={"grp": (grp + r) % n_grp}, device_id_type=MESH,
            )
            copy.start()
            tile_sends.append(copy)

    for band in range(bands):
        ka[band_slice(band), :] = jnp.dot(
            kp[band_slice(band), :], am[...], preferred_element_type=jnp.float32
        )

    number = 0
    for band in range(bands):
        width = -(-((band + 1) * rows) // 128) * 128
        total = s_loc[band, :, 0:width].astype(jnp.float32)
        for r in range(1, n_grp):
            tile_sends[number].wait_recv()
            number += 1
            total += s_in[r - 1, band, :, 0:width].astype(jnp.float32)
        low[band_slice(band), 0:width] = total / coef
    lower = low[...]
    row_band = lax.broadcasted_iota(jnp.int32, (slots, slots), 0) // rows
    column_band = lax.broadcasted_iota(jnp.int32, (slots, slots), 1) // rows
    ham[...] = jnp.where(row_band >= column_band, lower, lower.T).astype(jnp.bfloat16)

    returns = []
    for band in reversed(range(bands)):
        mult = jnp.dot(
            kp[band_slice(band), :], ham[...], preferred_element_type=jnp.float32
        ).astype(jnp.bfloat16)
        grad = ka[band_slice(band), :] - jnp.dot(mult, fm[...], preferred_element_type=jnp.float32)
        grad = jnp.where(live_mask(band), grad, jnp.float32(0.0))
        for t in reversed(range(group)):
            i = band * group + t
            g_buf[i] = grad[t * per:(t + 1) * per, :].astype(jnp.bfloat16)
            if i == 0:
                copy = pltpu.make_async_copy(g_buf.at[0], out_ref.at[dev], own_sem.at[0])
            else:
                copy = pltpu.make_async_remote_copy(
                    src_ref=g_buf.at[i], dst_ref=out_ref.at[dev],
                    send_sem=g_send.at[i], recv_sem=g_recv.at[dev],
                    device_id={"dev": sources[i]}, device_id_type=MESH,
                )
                returns.append(copy)
            copy.start()
            if i == 0:
                last_own = copy

    for copy in outgoing + tile_sends + returns:
        copy.wait_send()
    last_own.wait()
    for i in range(1, n_dev):
        pltpu.make_async_remote_copy(
            src_ref=g_buf.at[i], dst_ref=out_ref.at[sources[i]],
            send_sem=g_send.at[i], recv_sem=g_recv.at[sources[i]],
            device_id={"dev": sources[i]}, device_id_type=MESH,
        ).wait_recv()


def shards(n_grp, n_dev, functions, applied, kernel, live_counts, coef_counts):
    slots, coef = functions.shape
    per = slots // n_dev
    bands = min(BANDS, n_dev)
    rows = slots // bands
    pieces = (n_dev, per, coef)
    bf16, f32 = jnp.bfloat16, jnp.float32
    dma = pltpu.SemaphoreType.DMA
    anywhere = pl.BlockSpec(memory_space=pl.ANY)
    scalars = pl.BlockSpec(memory_space=pltpu.SMEM)
    result = pl.pallas_call(
        functools.partial(body, n_grp, n_dev),
        out_shape=jax.ShapeDtypeStruct(pieces, bf16),
        in_specs=[scalars, scalars, anywhere, anywhere, anywhere],
        out_specs=anywhere,
        scratch_shapes=[
            pltpu.VMEM(pieces, bf16), pltpu.VMEM(pieces, bf16), pltpu.VMEM((n_dev, per, slots), bf16),
            pltpu.VMEM((slots, coef), bf16), pltpu.VMEM((slots, coef), bf16),
            pltpu.VMEM((slots, slots), bf16), pltpu.VMEM((slots, coef), f32),
            pltpu.VMEM((bands, rows, slots), bf16), pltpu.VMEM((n_grp - 1, bands, rows, slots), bf16),
            pltpu.VMEM((slots, slots), f32), pltpu.VMEM((slots, slots), bf16),
            pltpu.VMEM(pieces, bf16),
            dma((n_dev,)), dma((n_dev,)), dma((n_dev,)), dma((n_dev,)),
            dma((n_grp - 1, bands)), dma((n_grp - 1, bands)),
            dma((n_dev,)), dma((n_dev,)), dma((n_dev,)), dma((2,)),
        ],
        compiler_params=pltpu.CompilerParams(
            collective_id=0, has_side_effects=True, vmem_limit_bytes=60 * 1024 * 1024
        ),
        name="region_step",
    )(
        live_counts, coef_counts, functions.reshape(pieces), applied.reshape(pieces),
        kernel.reshape(n_dev, per, slots),
    )
    return result.reshape(slots, coef)


def solution(mesh):
    placed = (P("dev", "grp"), P("dev", "grp"), P("dev", None), P("dev", None), P("grp", "dev"))
    return jax.shard_map(
        functools.partial(shards, mesh.shape["grp"], mesh.shape["dev"]),
        mesh=mesh, in_specs=placed, out_specs=P("dev", "grp"), check_vma=False,
    )
```

```python
import functools

import jax
import jax.numpy as jnp
from jax import lax
from jax.experimental import pallas as pl
from jax.experimental.pallas import tpu as pltpu
from jax.sharding import PartitionSpec as P

MESH = pl.DeviceIdType.MESH
CORES = 2
BANDS = 8


def arrival_orders(chips):
    half = chips // 2
    return [
        sorted(range(chips), key=lambda s: (abs(s - z), (s < half) != (z < half), s)) for z in range(chips)
    ]


def pick(index, values):
    if all(v == values[0] for v in values):
        return values[0]
    found = jnp.int32(values[0])
    for k in range(1, len(values)):
        found = jnp.where(index == k, jnp.int32(values[k]), found)
    return found


def body(
    n_grp, n_dev, live_ref, coef_ref, f_hbm, a_hbm, k_hbm, out_ref,
    land_f, land_a, land_k, fm, am, kp, ka, s_loc, s_in, low, ham, g_buf,
    f_send, f_recv, a_send, a_recv, s_send, s_recv, g_send, g_recv, k_sem, own_sem,
):
    per, coef = f_hbm.shape[1:]
    slots = n_dev * per
    chips = n_dev // CORES
    bands = min(BANDS, n_dev)
    group = n_dev // bands
    rows = group * per
    grp, dev = lax.axis_index("grp"), lax.axis_index("dev")
    chip, core = dev // CORES, dev % CORES
    other = 1 - core
    orders = arrival_orders(chips)

    sources = []
    for p in range(chips):
        z = pick(chip, [orders[k][p] for k in range(chips)])
        sources += [z * CORES + core, z * CORES + other]
    sends = []
    for p in range(1, chips):
        z = pick(chip, [orders[k][p] for k in range(chips)])
        spot = pick(chip, [orders[orders[k][p]].index(k) for k in range(chips)])
        sends += [(z * CORES + core, spot * CORES), (z * CORES + other, spot * CORES + 1)]
    sends.append((chip * CORES + other, 1))

    k_copies = [
        pltpu.make_async_copy(k_hbm.at[sources[i]], land_k.at[i], k_sem.at[i]) for i in range(n_dev)
    ]
    own = [
        pltpu.make_async_copy(f_hbm.at[dev], land_f.at[0], own_sem.at[0]),
        pltpu.make_async_copy(a_hbm.at[dev], land_a.at[0], own_sem.at[1]),
    ]

    barrier = pltpu.get_barrier_semaphore()
    for r in range(1, n_dev):
        pl.semaphore_signal(barrier, inc=1, device_id={"dev": (dev + r) % n_dev}, device_id_type=MESH)
    for r in range(1, n_grp):
        pl.semaphore_signal(barrier, inc=1, device_id={"grp": (grp + r) % n_grp}, device_id_type=MESH)
    for copy in own + k_copies:
        copy.start()
    pl.semaphore_wait(barrier, n_dev + n_grp - 2)

    outgoing = []
    for number, (target, spot) in enumerate(sends):
        for src, dst, ss, rs in ((f_hbm, land_f, f_send, f_recv), (a_hbm, land_a, a_send, a_recv)):
            copy = pltpu.make_async_remote_copy(
                src_ref=src.at[target], dst_ref=dst.at[spot],
                send_sem=ss.at[number], recv_sem=rs.at[spot],
                device_id={"dev": target}, device_id_type=MESH,
            )
            copy.start()
            outgoing.append(copy)

    def flat(ref, band):
        pieces = [ref[band * group + t].astype(jnp.float32) for t in range(group)]
        return jnp.concatenate(pieces, axis=0) if group > 1 else pieces[0]

    def band_slice(band):
        return pl.ds(band * rows, rows)

    column = lax.broadcasted_iota(jnp.int32, (1, slots), 1)
    target_row = jnp.zeros((1, slots), jnp.int32)
    for i in range(n_dev):
        inside = (column >= i * per) & (column < (i + 1) * per)
        target_row = jnp.where(inside, column + (sources[i] - i) * per, target_row)
    onehot = (lax.broadcasted_iota(jnp.int32, (slots, slots), 0) == target_row)
    ham[...] = jnp.where(onehot, jnp.float32(1.0), jnp.float32(0.0)).astype(jnp.bfloat16)
    for copy in k_copies:
        copy.wait()
    for band in range(bands):
        kp[band_slice(band), :] = jnp.dot(
            flat(land_k, band).astype(jnp.bfloat16), ham[...], preferred_element_type=jnp.float32
        ).astype(jnp.bfloat16)

    coef_live = lax.broadcasted_iota(jnp.int32, (rows, coef), 1) < coef_ref[0, 0]
    rank = lax.broadcasted_iota(jnp.int32, (rows, coef), 0)

    def live_mask(band):
        live = None
        for t in range(group):
            count = live_ref[0, sources[band * group + t]]
            inside = (rank >= t * per) & (rank < t * per + jnp.minimum(count, per))
            live = inside if live is None else live | inside
        return live & coef_live

    low[...] = jnp.zeros_like(low)
    contract = (((1,), (1,)), ((), ()))
    steps = n_grp.bit_length() - 1
    half_rows = rows // 2

    def width_of(band):
        return -(-((band + 1) * rows) // 128) * 128

    def tile_copy(step, band, half):
        bit = 2 ** (step if half == 0 else steps - 1 - step)
        peer = grp + bit * (1 - 2 * ((grp // bit) % 2))
        place = (step, band, pl.ds(half * half_rows, half_rows), pl.ds(0, width_of(band)))
        return pltpu.make_async_remote_copy(
            src_ref=s_loc.at[place], dst_ref=s_in.at[place],
            send_sem=s_send.at[step, band, half], recv_sem=s_recv.at[step, band, half],
            device_id={"grp": peer}, device_id_type=MESH,
        )

    def advance(step, band):
        wide = pl.ds(0, width_of(band))
        for half in range(2):
            here = pl.ds(half * half_rows, half_rows)
            tile_copy(step, band, half).wait_recv()
            total = s_loc[step, band, here, wide].astype(jnp.float32)
            total += s_in[step, band, here, wide].astype(jnp.float32)
            if step + 1 < steps:
                s_loc[step + 1, band, here, wide] = total.astype(jnp.bfloat16)
                tile_copy(step + 1, band, half).start()
            else:
                low[pl.ds(band * rows + half * half_rows, half_rows), wide] = total / coef

    def arrive(band):
        for i in range(band * group, (band + 1) * group):
            if i == 0:
                own[0].wait()
                own[1].wait()
                continue
            for src, dst, ss, rs in ((f_hbm, land_f, f_send, f_recv), (a_hbm, land_a, a_send, a_recv)):
                pltpu.make_async_remote_copy(
                    src_ref=src.at[0], dst_ref=dst.at[i], send_sem=ss.at[0], recv_sem=rs.at[i],
                    device_id={"dev": sources[i]}, device_id_type=MESH,
                ).wait_recv()
        mask = live_mask(band)
        f_new = jnp.where(mask, flat(land_f, band), jnp.float32(0.0)).astype(jnp.bfloat16)
        a_new = jnp.where(mask, flat(land_a, band), jnp.float32(0.0)).astype(jnp.bfloat16)
        fm[band_slice(band), :] = f_new
        am[band_slice(band), :] = a_new
        upto = (band + 1) * rows
        tile = lax.dot_general(f_new, am[0:upto, :], contract, preferred_element_type=jnp.float32)
        tile += lax.dot_general(a_new, fm[0:upto, :], contract, preferred_element_type=jnp.float32)
        low[band_slice(band), 0:upto] = 0.5 * tile
        wide = pl.ds(0, width_of(band))
        s_loc[0, band, :, wide] = low[band_slice(band), wide].astype(jnp.bfloat16)
        for half in range(2):
            tile_copy(0, band, half).start()

    def multiply_kernel(first, last):
        for band in range(first, last):
            ka[band_slice(band), :] = jnp.dot(
                kp[band_slice(band), :], am[...], preferred_element_type=jnp.float32
            )

    def mirror(start, size):
        lower = low[:, start:start + size]
        upper = low[start:start + size, :].T
        row_band = lax.broadcasted_iota(jnp.int32, (slots, size), 0) // rows
        column_band = (lax.broadcasted_iota(jnp.int32, (slots, size), 1) + start) // rows
        ham[:, start:start + size] = jnp.where(row_band >= column_band, lower, upper).astype(jnp.bfloat16)

    for turn in range(bands + steps):
        if turn < bands:
            arrive(turn)
        for step in range(steps):
            if 0 <= turn - 1 - step < bands:
                advance(step, turn - 1 - step)
        if turn == bands - 1:
            multiply_kernel(0, bands // 2)
        if turn == bands + steps - 2:
            mirror(0, slots)
            multiply_kernel(bands // 2, bands)
    edge = (slots - rows) // 128 * 128
    ham[band_slice(bands - 1), :] = low[band_slice(bands - 1), :].astype(jnp.bfloat16)
    mirror(edge, slots - edge)

    returns = []
    for band in reversed(range(bands)):
        mult = jnp.dot(
            kp[band_slice(band), :], ham[...], preferred_element_type=jnp.float32
        ).astype(jnp.bfloat16)
        grad = ka[band_slice(band), :] - jnp.dot(mult, fm[...], preferred_element_type=jnp.float32)
        grad = jnp.where(live_mask(band), grad, jnp.float32(0.0))
        for t in reversed(range(group)):
            i = band * group + t
            g_buf[i] = grad[t * per:(t + 1) * per, :].astype(jnp.bfloat16)
            if i == 0:
                copy = pltpu.make_async_copy(g_buf.at[0], out_ref.at[dev], own_sem.at[0])
            else:
                copy = pltpu.make_async_remote_copy(
                    src_ref=g_buf.at[i], dst_ref=out_ref.at[dev],
                    send_sem=g_send.at[i], recv_sem=g_recv.at[dev],
                    device_id={"dev": sources[i]}, device_id_type=MESH,
                )
                returns.append(copy)
            copy.start()
            if i == 0:
                last_own = copy

    tile_sends = [
        tile_copy(step, band, half) for step in range(steps) for band in range(bands) for half in range(2)
    ]
    for copy in outgoing + tile_sends + returns:
        copy.wait_send()
    last_own.wait()
    for i in range(1, n_dev):
        pltpu.make_async_remote_copy(
            src_ref=g_buf.at[i], dst_ref=out_ref.at[sources[i]],
            send_sem=g_send.at[i], recv_sem=g_recv.at[sources[i]],
            device_id={"dev": sources[i]}, device_id_type=MESH,
        ).wait_recv()


def shards(n_grp, n_dev, functions, applied, kernel, live_counts, coef_counts):
    slots, coef = functions.shape
    per = slots // n_dev
    bands = min(BANDS, n_dev)
    rows = slots // bands
    pieces = (n_dev, per, coef)
    steps = n_grp.bit_length() - 1
    bf16, f32 = jnp.bfloat16, jnp.float32
    dma = pltpu.SemaphoreType.DMA
    anywhere = pl.BlockSpec(memory_space=pl.ANY)
    scalars = pl.BlockSpec(memory_space=pltpu.SMEM)
    result = pl.pallas_call(
        functools.partial(body, n_grp, n_dev),
        out_shape=jax.ShapeDtypeStruct(pieces, bf16),
        in_specs=[scalars, scalars, anywhere, anywhere, anywhere],
        out_specs=anywhere,
        scratch_shapes=[
            pltpu.VMEM(pieces, bf16), pltpu.VMEM(pieces, bf16), pltpu.VMEM((n_dev, per, slots), bf16),
            pltpu.VMEM((slots, coef), bf16), pltpu.VMEM((slots, coef), bf16),
            pltpu.VMEM((slots, slots), bf16), pltpu.VMEM((slots, coef), f32),
            pltpu.VMEM((steps, bands, rows, slots), bf16), pltpu.VMEM((steps, bands, rows, slots), bf16),
            pltpu.VMEM((slots, slots), f32), pltpu.VMEM((slots, slots), bf16),
            pltpu.VMEM(pieces, bf16),
            dma((n_dev,)), dma((n_dev,)), dma((n_dev,)), dma((n_dev,)),
            dma((steps, bands, 2)), dma((steps, bands, 2)),
            dma((n_dev,)), dma((n_dev,)), dma((n_dev,)), dma((2,)),
        ],
        compiler_params=pltpu.CompilerParams(
            collective_id=0, has_side_effects=True, vmem_limit_bytes=60 * 1024 * 1024
        ),
        name="region_step",
    )(
        live_counts, coef_counts, functions.reshape(pieces), applied.reshape(pieces),
        kernel.reshape(n_dev, per, slots),
    )
    return result.reshape(slots, coef)


def solution(mesh):
    placed = (P("dev", "grp"), P("dev", "grp"), P("dev", None), P("dev", None), P("grp", "dev"))
    return jax.shard_map(
        functools.partial(shards, mesh.shape["grp"], mesh.shape["dev"]),
        mesh=mesh, in_specs=placed, out_specs=P("dev", "grp"), check_vma=False,
    )
```

```python
import functools

import jax
import jax.numpy as jnp
from jax import lax
from jax.experimental import pallas as pl
from jax.experimental.pallas import tpu as pltpu
from jax.sharding import PartitionSpec as P

MESH = pl.DeviceIdType.MESH
CORES = 2
BANDS = 8


def arrival_orders(chips):
    half = chips // 2
    return [
        sorted(range(chips), key=lambda s: (s != z, -abs(s - z), (s < half) != (z < half), s)) for z in range(chips)
    ]


def pick(index, values):
    if all(v == values[0] for v in values):
        return values[0]
    found = jnp.int32(values[0])
    for k in range(1, len(values)):
        found = jnp.where(index == k, jnp.int32(values[k]), found)
    return found


def body(
    n_grp, n_dev, live_ref, coef_ref, f_hbm, a_hbm, k_hbm, out_ref,
    land_f, land_a, land_k, fm, am, kp, ka, s_loc, s_in, low, ham, g_buf,
    f_send, f_recv, a_send, a_recv, s_send, s_recv, g_send, g_recv, k_sem, own_sem,
):
    per, coef = f_hbm.shape[1:]
    slots = n_dev * per
    chips = n_dev // CORES
    bands = min(BANDS, n_dev)
    group = n_dev // bands
    rows = group * per
    grp, dev = lax.axis_index("grp"), lax.axis_index("dev")
    chip, core = dev // CORES, dev % CORES
    other = 1 - core
    orders = arrival_orders(chips)

    sources = []
    for p in range(chips):
        z = pick(chip, [orders[k][p] for k in range(chips)])
        sources += [z * CORES + core, z * CORES + other]
    sends = []
    for p in range(1, chips):
        z = pick(chip, [orders[k][p] for k in range(chips)])
        spot = pick(chip, [orders[orders[k][p]].index(k) for k in range(chips)])
        sends += [(z * CORES + core, spot * CORES), (z * CORES + other, spot * CORES + 1)]
    sends.append((chip * CORES + other, 1))

    k_copies = [
        pltpu.make_async_copy(k_hbm.at[sources[i]], land_k.at[i], k_sem.at[i]) for i in range(n_dev)
    ]
    own = [
        pltpu.make_async_copy(f_hbm.at[dev], land_f.at[0], own_sem.at[0]),
        pltpu.make_async_copy(a_hbm.at[dev], land_a.at[0], own_sem.at[1]),
    ]

    barrier = pltpu.get_barrier_semaphore()
    for r in range(1, n_dev):
        pl.semaphore_signal(barrier, inc=1, device_id={"dev": (dev + r) % n_dev}, device_id_type=MESH)
    for r in range(1, n_grp):
        pl.semaphore_signal(barrier, inc=1, device_id={"grp": (grp + r) % n_grp}, device_id_type=MESH)
    for copy in own + k_copies:
        copy.start()
    pl.semaphore_wait(barrier, n_dev + n_grp - 2)

    outgoing = []
    for number, (target, spot) in enumerate(sends):
        for src, dst, ss, rs in ((f_hbm, land_f, f_send, f_recv), (a_hbm, land_a, a_send, a_recv)):
            copy = pltpu.make_async_remote_copy(
                src_ref=src.at[target], dst_ref=dst.at[spot],
                send_sem=ss.at[number], recv_sem=rs.at[spot],
                device_id={"dev": target}, device_id_type=MESH,
            )
            copy.start()
            outgoing.append(copy)

    def flat(ref, band):
        pieces = [ref[band * group + t].astype(jnp.float32) for t in range(group)]
        return jnp.concatenate(pieces, axis=0) if group > 1 else pieces[0]

    def band_slice(band):
        return pl.ds(band * rows, rows)

    column = lax.broadcasted_iota(jnp.int32, (1, slots), 1)
    target_row = jnp.zeros((1, slots), jnp.int32)
    for i in range(n_dev):
        inside = (column >= i * per) & (column < (i + 1) * per)
        target_row = jnp.where(inside, column + (sources[i] - i) * per, target_row)
    onehot = (lax.broadcasted_iota(jnp.int32, (slots, slots), 0) == target_row)
    ham[...] = jnp.where(onehot, jnp.float32(1.0), jnp.float32(0.0)).astype(jnp.bfloat16)
    for copy in k_copies:
        copy.wait()
    for band in range(bands):
        kp[band_slice(band), :] = jnp.dot(
            flat(land_k, band).astype(jnp.bfloat16), ham[...], preferred_element_type=jnp.float32
        ).astype(jnp.bfloat16)

    coef_live = lax.broadcasted_iota(jnp.int32, (rows, coef), 1) < coef_ref[0, 0]
    rank = lax.broadcasted_iota(jnp.int32, (rows, coef), 0)

    def live_mask(band):
        live = None
        for t in range(group):
            count = live_ref[0, sources[band * group + t]]
            inside = (rank >= t * per) & (rank < t * per + jnp.minimum(count, per))
            live = inside if live is None else live | inside
        return live & coef_live

    low[...] = jnp.zeros_like(low)
    contract = (((1,), (1,)), ((), ()))
    steps = n_grp.bit_length() - 1
    half_rows = rows // 2

    def width_of(band):
        return -(-((band + 1) * rows) // 128) * 128

    def tile_copy(step, band, half):
        bit = 2 ** (step if half == 0 else steps - 1 - step)
        peer = grp + bit * (1 - 2 * ((grp // bit) % 2))
        place = (step, band, pl.ds(half * half_rows, half_rows), pl.ds(0, width_of(band)))
        return pltpu.make_async_remote_copy(
            src_ref=s_loc.at[place], dst_ref=s_in.at[place],
            send_sem=s_send.at[step, band, half], recv_sem=s_recv.at[step, band, half],
            device_id={"grp": peer}, device_id_type=MESH,
        )

    def advance(step, band):
        wide = pl.ds(0, width_of(band))
        for half in range(2):
            here = pl.ds(half * half_rows, half_rows)
            tile_copy(step, band, half).wait_recv()
            total = s_loc[step, band, here, wide].astype(jnp.float32)
            total += s_in[step, band, here, wide].astype(jnp.float32)
            if step + 1 < steps:
                s_loc[step + 1, band, here, wide] = total.astype(jnp.bfloat16)
                tile_copy(step + 1, band, half).start()
            else:
                low[pl.ds(band * rows + half * half_rows, half_rows), wide] = total / coef

    def arrive(band):
        for i in range(band * group, (band + 1) * group):
            if i == 0:
                own[0].wait()
                own[1].wait()
                continue
            for src, dst, ss, rs in ((f_hbm, land_f, f_send, f_recv), (a_hbm, land_a, a_send, a_recv)):
                pltpu.make_async_remote_copy(
                    src_ref=src.at[0], dst_ref=dst.at[i], send_sem=ss.at[0], recv_sem=rs.at[i],
                    device_id={"dev": sources[i]}, device_id_type=MESH,
                ).wait_recv()
        mask = live_mask(band)
        f_new = jnp.where(mask, flat(land_f, band), jnp.float32(0.0)).astype(jnp.bfloat16)
        a_new = jnp.where(mask, flat(land_a, band), jnp.float32(0.0)).astype(jnp.bfloat16)
        fm[band_slice(band), :] = f_new
        am[band_slice(band), :] = a_new
        upto = (band + 1) * rows
        tile = lax.dot_general(f_new, am[0:upto, :], contract, preferred_element_type=jnp.float32)
        tile += lax.dot_general(a_new, fm[0:upto, :], contract, preferred_element_type=jnp.float32)
        low[band_slice(band), 0:upto] = 0.5 * tile
        wide = pl.ds(0, width_of(band))
        s_loc[0, band, :, wide] = low[band_slice(band), wide].astype(jnp.bfloat16)
        for half in range(2):
            tile_copy(0, band, half).start()

    def multiply_kernel(first, last):
        for band in range(first, last):
            ka[band_slice(band), :] = jnp.dot(
                kp[band_slice(band), :], am[...], preferred_element_type=jnp.float32
            )

    def mirror(start, size):
        lower = low[:, start:start + size]
        upper = low[start:start + size, :].T
        row_band = lax.broadcasted_iota(jnp.int32, (slots, size), 0) // rows
        column_band = (lax.broadcasted_iota(jnp.int32, (slots, size), 1) + start) // rows
        ham[:, start:start + size] = jnp.where(row_band >= column_band, lower, upper).astype(jnp.bfloat16)

    for turn in range(bands + steps):
        if turn < bands:
            arrive(turn)
        for step in range(steps):
            if 0 <= turn - 1 - step < bands:
                advance(step, turn - 1 - step)
        if turn == bands - 1:
            multiply_kernel(0, bands // 2)
        if turn == bands + steps - 2:
            mirror(0, slots)
            multiply_kernel(bands // 2, bands)
    edge = (slots - rows) // 128 * 128
    ham[band_slice(bands - 1), :] = low[band_slice(bands - 1), :].astype(jnp.bfloat16)
    mirror(edge, slots - edge)

    returns = []
    own_bands = -(-CORES // group)
    for band in [*range(own_bands, bands), *reversed(range(own_bands))]:
        mult = jnp.dot(
            kp[band_slice(band), :], ham[...], preferred_element_type=jnp.float32
        ).astype(jnp.bfloat16)
        grad = ka[band_slice(band), :] - jnp.dot(mult, fm[...], preferred_element_type=jnp.float32)
        grad = jnp.where(live_mask(band), grad, jnp.float32(0.0))
        for t in range(group):
            i = band * group + t
            g_buf[i] = grad[t * per:(t + 1) * per, :].astype(jnp.bfloat16)
            if i == 0:
                copy = pltpu.make_async_copy(g_buf.at[0], out_ref.at[dev], own_sem.at[0])
            else:
                copy = pltpu.make_async_remote_copy(
                    src_ref=g_buf.at[i], dst_ref=out_ref.at[dev],
                    send_sem=g_send.at[i], recv_sem=g_recv.at[dev],
                    device_id={"dev": sources[i]}, device_id_type=MESH,
                )
                returns.append(copy)
            copy.start()
            if i == 0:
                last_own = copy

    tile_sends = [
        tile_copy(step, band, half) for step in range(steps) for band in range(bands) for half in range(2)
    ]
    for copy in outgoing + tile_sends + returns:
        copy.wait_send()
    last_own.wait()
    for i in range(1, n_dev):
        pltpu.make_async_remote_copy(
            src_ref=g_buf.at[i], dst_ref=out_ref.at[sources[i]],
            send_sem=g_send.at[i], recv_sem=g_recv.at[sources[i]],
            device_id={"dev": sources[i]}, device_id_type=MESH,
        ).wait_recv()


def shards(n_grp, n_dev, functions, applied, kernel, live_counts, coef_counts):
    slots, coef = functions.shape
    per = slots // n_dev
    bands = min(BANDS, n_dev)
    rows = slots // bands
    pieces = (n_dev, per, coef)
    steps = n_grp.bit_length() - 1
    bf16, f32 = jnp.bfloat16, jnp.float32
    dma = pltpu.SemaphoreType.DMA
    anywhere = pl.BlockSpec(memory_space=pl.ANY)
    scalars = pl.BlockSpec(memory_space=pltpu.SMEM)
    result = pl.pallas_call(
        functools.partial(body, n_grp, n_dev),
        out_shape=jax.ShapeDtypeStruct(pieces, bf16),
        in_specs=[scalars, scalars, anywhere, anywhere, anywhere],
        out_specs=anywhere,
        scratch_shapes=[
            pltpu.VMEM(pieces, bf16), pltpu.VMEM(pieces, bf16), pltpu.VMEM((n_dev, per, slots), bf16),
            pltpu.VMEM((slots, coef), bf16), pltpu.VMEM((slots, coef), bf16),
            pltpu.VMEM((slots, slots), bf16), pltpu.VMEM((slots, coef), f32),
            pltpu.VMEM((steps, bands, rows, slots), bf16), pltpu.VMEM((steps, bands, rows, slots), bf16),
            pltpu.VMEM((slots, slots), f32), pltpu.VMEM((slots, slots), bf16),
            pltpu.VMEM(pieces, bf16),
            dma((n_dev,)), dma((n_dev,)), dma((n_dev,)), dma((n_dev,)),
            dma((steps, bands, 2)), dma((steps, bands, 2)),
            dma((n_dev,)), dma((n_dev,)), dma((n_dev,)), dma((2,)),
        ],
        compiler_params=pltpu.CompilerParams(
            collective_id=0, has_side_effects=True, vmem_limit_bytes=60 * 1024 * 1024
        ),
        name="region_step",
    )(
        live_counts, coef_counts, functions.reshape(pieces), applied.reshape(pieces),
        kernel.reshape(n_dev, per, slots),
    )
    return result.reshape(slots, coef)


def solution(mesh):
    placed = (P("dev", "grp"), P("dev", "grp"), P("dev", None), P("dev", None), P("grp", "dev"))
    return jax.shard_map(
        functools.partial(shards, mesh.shape["grp"], mesh.shape["dev"]),
        mesh=mesh, in_specs=placed, out_specs=P("dev", "grp"), check_vma=False,
    )
```
